32 devices in a mesh: depth: 2 (over y), row: 4 (over x, core), col: 4 (over z).
Axes of the slice: x: 2, y: 2, z: 4, core: 2. Of those that a mesh axis runs over, the one named last changes fastest.
Arguments:
- volume: float32 [2, 1024, 1024], P('depth', 'row', 'col'), may hold values from -6 to 6
- psf_spec: float32 [2, 2, 1024, 1024], P(None, 'depth', 'row', 'col'), may hold values from -1.5 to 1.5
- measured: float32 [1024, 1024], P('row', 'col'), may hold values from -6 to 6
- dual: float32 [3, 2, 1024, 1024], P(None, 'depth', 'row', 'col'), may hold values from -3 to 3
Outputs:
- updated: float32 [2, 1024, 1024], P('depth', 'row', 'col')
- shrunk: float32 [3, 2, 1024, 1024], P(None, 'depth', 'row', 'col')
- dual_next: float32 [3, 2, 1024, 1024], P(None, 'depth', 'row', 'col')
The draws below stay inside these ranges and needn't reach their ends.
All inputs are finite; a program needn't handle non-finite values.
Results may differ from the reference program's by a relative error of at most 0.00005.
Values sent between devices are 32-bit elements; how exact they have to be, the bound alone decides.
A program may use at most 64 MiB of HBM per device.

```python
import jax
import jax.numpy as jnp
from jax import lax

H = 1024
W = 1024
Z = 2


def block_scale(own_key, extent, shards, least, largest):
    level = 1.0
    for axis_at, parts in shards:
        draws = jax.random.uniform(jax.random.fold_in(jax.random.fold_in(own_key, 6), axis_at), (parts,), jnp.float32, least / len(shards), largest / len(shards))
        level = level * jnp.repeat(jnp.exp(draws), extent[axis_at] // parts).reshape((-1,) + (1,) * (len(extent) - 1 - axis_at))
    return level


def normal_values(own_key, shape, width, reach, shards=(), kind=jnp.bfloat16):
    array = jax.random.normal(own_key, shape, jnp.float32) * width
    if len(shards) > 0:
        array = block_scale(own_key, shape, shards, -0.22, 0.18) * array
    return jnp.clip(array, min=-reach, max=reach).astype(kind)


def setup_inputs(seed: int = 0) -> dict:
    keys = jax.random.split(jax.random.key(seed), 5)
    return {
        "volume": normal_values(keys[0], (Z, H, W), 1.0, 6.0, ((0, 2), (1, 4), (2, 4)), jnp.float32),
        "psf_spec": normal_values(keys[1], (2, Z, H, W), 0.25, 1.5, ((1, 2), (2, 4), (3, 4)), jnp.float32),
        "measured": normal_values(keys[2], (H, W), 1.0, 6.0, ((0, 4), (1, 4)), jnp.float32),
        "dual": normal_values(keys[3], (3, Z, H, W), 0.5, 3.0, ((1, 2), (2, 4), (3, 4)), jnp.float32),
    }


step_size = 1.0
shrink_level = 0.5


def reference(volume, psf_spec, measured, dual):
    kernel = lax.complex(psf_spec[0], psf_spec[1])
    spectra = jnp.fft.fft2(volume)
    sensor_image = jnp.real(jnp.fft.ifft2(jnp.sum(kernel * spectra, axis=0)))
    row_ids = jnp.arange(H, dtype=jnp.int32)
    col_ids = jnp.arange(W, dtype=jnp.int32)
    inside = ((row_ids >= H // 4) & (row_ids < 3 * H // 4))[:, None] & ((col_ids >= W // 4) & (col_ids < 3 * W // 4))[None, :]
    residual_map = jnp.where(inside, sensor_image - measured, jnp.zeros_like(measured))
    adjoint = jnp.real(jnp.fft.ifft2(jnp.conj(kernel) * jnp.fft.fft2(residual_map)[None]))
    updated = volume - step_size * adjoint
    diff_depth = jnp.concatenate([updated[1:] - updated[:-1], jnp.zeros_like(updated[:1])], axis=0)
    diff_rows = jnp.concatenate([updated[:, 1:] - updated[:, :-1], jnp.zeros_like(updated[:, :1])], axis=1)
    diff_cols = jnp.concatenate([updated[:, :, 1:] - updated[:, :, :-1], jnp.zeros_like(updated[:, :, :1])], axis=2)
    combined = jnp.stack([diff_depth, diff_rows, diff_cols]) + dual
    dual_next = jnp.clip(combined, -shrink_level, shrink_level)
    return updated, combined - dual_next, dual_next
```

```python
import functools

import jax
import jax.numpy as jnp
import numpy as np
from jax import lax
from jax.experimental import pallas as pl
from jax.experimental.pallas import tpu as pltpu
from jax.sharding import PartitionSpec as P

step_size = 1.0
shrink_level = 0.5
MESH = pl.DeviceIdType.MESH
highest = lax.Precision.HIGHEST


def dot(a, b):
    return lax.dot_general(a, b, (((1,), (0,)), ((), ())), precision=highest, preferred_element_type=jnp.float32)


def dot_nt(a, b):
    return lax.dot_general(a, b, (((1,), (1,)), ((), ())), precision=highest, preferred_element_type=jnp.float32)


def root(count, n):
    value = np.exp(-2j * np.pi * (n % count) / count)
    real, imag = float(value.real), float(value.imag)
    real = round(real) if abs(real - round(real)) < 1e-12 else real
    imag = round(imag) if abs(imag - round(imag)) < 1e-12 else imag
    return float(real), float(imag)


def add_scaled(total, scale, value):
    if scale == 0.0:
        return total
    if total is None:
        return value if scale == 1.0 else (-value if scale == -1.0 else scale * value)
    if scale == 1.0:
        return total + value
    if scale == -1.0:
        return total - value
    return total + scale * value


def spin(u):
    half = u.shape[-1] // 2
    lane = lax.broadcasted_iota(jnp.int32, u.shape, u.ndim - 1)
    rolled = pltpu.roll(u, half, u.ndim - 1)
    return jnp.where(lane < half, -rolled, rolled)


def body(D, R, C, hb, wb,
         vol, psf, meas, dual, mat_w, mat_h, tw_w, tw_h,
         upd, shr, dnx,
         r_vol, k_send, k_recv, r_meas, s1, r1, s2, r2, s3, r3, s4, r4, s5, r5, ups, h_dep, h_row, h_col,
         sm_vol, sm_k, sm_meas, sm1, sm2s, sm2r, sm3s, sm3r, sm4, sm5, sm_h):
    H, W = R * hb, C * wb
    rows, q = hb // C, wb // R
    rs = rows // D
    lo, hi, lo_c, hi_c = R // 4, 3 * R // 4, C // 4, 3 * C // 4
    NR = hi - lo
    N, n16, NO = D * R * C, R * C, D * NR * C
    d, r, c = lax.axis_index("depth"), lax.axis_index("row"), lax.axis_index("col")
    me16 = r * C + c
    me = d * n16 + me16

    def ids(t):
        return {"depth": t // n16, "row": (t // C) % R, "col": t % C}

    barrier = pltpu.get_barrier_semaphore()

    def greet(o, _):
        pl.semaphore_signal(barrier, inc=1, device_id=ids(lax.rem(me + o, N)), device_id_type=MESH)
        return 0

    lax.fori_loop(1, N, greet, 0)

    def rc(src, dst, ss, rsm, dev):
        return pltpu.make_async_remote_copy(src_ref=src, dst_ref=dst, send_sem=ss, recv_sem=rsm, device_id=dev, device_id_type=MESH)

    def loop(lower, upper, f):
        def g(i, x):
            f(i)
            return x
        lax.fori_loop(lower, upper, g, 0)

    class A2A:
        def __init__(self, n, pos, dev, src, recv, sems):
            self.n, self.pos, self.dev, self.src, self.recv, self.sems = n, pos, dev, src, recv, sems

        def start(self):
            def go(o):
                t = lax.rem(self.pos + o, self.n)
                rc(self.src(t), self.recv.at[self.pos], self.sems.at[0, t], self.sems.at[1, self.pos], self.dev(t)).start()
            loop(1, self.n, go)

        def wait(self):
            def go(o):
                t = lax.rem(self.pos + o, self.n)
                rc(self.src(t), self.recv.at[t], self.sems.at[0, t], self.sems.at[1, t], self.dev(t)).wait()
            loop(1, self.n, go)

    col_dev = lambda t: {"col": t}
    row_dev = lambda t: {"row": t}
    all_dev = lambda t: {"row": t // C, "col": lax.rem(t, C)}

    x_vol = A2A(C, c, col_dev, lambda t: vol.at[t], r_vol, sm_vol)
    x_k = A2A(R, r, row_dev, lambda t: k_send.at[t], k_recv, sm_k)
    x_meas = A2A(C, c, col_dev, lambda t: meas.at[t, d], r_meas, sm_meas)
    x1 = A2A(n16, me16, all_dev, lambda t: s1.at[t], r1, sm1)
    x4 = A2A(n16, me16, all_dev, lambda t: s4.at[t], r4, sm4)
    x5 = A2A(C, c, col_dev, lambda t: s5.at[t], r5, sm5)

    pl.semaphore_wait(barrier, N - 1)
    x_vol.start()
    r_vol[c] = vol[c]

    kin = jnp.concatenate([psf[0], psf[1]], axis=1)
    i0 = lax.broadcasted_iota(jnp.int32, (2 * wb, 2 * wb), 0)
    i1 = lax.broadcasted_iota(jnp.int32, (2 * wb, 2 * wb), 1)
    target = (lax.rem(i1, 2 * q) // q) * wb + R * lax.rem(i1, q) + i1 // (2 * q)
    perm_c = jnp.where(i0 == target, 1.0, 0.0).astype(jnp.float32)
    j0 = lax.broadcasted_iota(jnp.int32, (hb, hb), 0)
    j1 = lax.broadcasted_iota(jnp.int32, (hb, hb), 1)
    t_rows = hb // R
    perm_r = jnp.where(j1 == R * lax.rem(j0, t_rows) + j0 // t_rows, 1.0, 0.0).astype(jnp.float32)
    kk = dot(perm_r, dot(kin, perm_c))
    for j in range(R):
        k_send[j] = kk[:, 2 * q * j:2 * q * (j + 1)]
    x_meas.start()
    r_meas[c] = meas[c, d]

    def fwd_w(blocks, first):
        tre, tim = [], []
        for k1 in range(C):
            yr = yi = None
            for i, blk in enumerate(blocks):
                a, b = root(C, (first + i) * k1)
                yr, yi = add_scaled(yr, a, blk), add_scaled(yi, b, blk)
            ct, st = tw_w[0, k1:k1 + 1, :], tw_w[1, k1:k1 + 1, :]
            if yi is None:
                tre.append(yr * ct)
                tim.append(yr * st)
            else:
                tre.append(yr * ct - yi * st)
                tim.append(yr * st + yi * ct)
        both = jnp.concatenate([jnp.concatenate(tre, 0), jnp.concatenate(tim, 0)], 1)
        return dot(both, mat_w[...])

    def inv_w(z, count, first, last):
        g = dot_nt(z, mat_w[...]) * (1.0 / W)
        gr, gi = [], []
        for k1 in range(C):
            a = g[k1 * count:(k1 + 1) * count, :wb]
            b = g[k1 * count:(k1 + 1) * count, wb:]
            ct, st = tw_w[0, k1:k1 + 1, :], tw_w[1, k1:k1 + 1, :]
            gr.append(a * ct + b * st)
            gi.append(b * ct - a * st)
        out = []
        for n1 in range(first, last):
            total = None
            for k1 in range(C):
                a, b = root(C, n1 * k1)
                total = add_scaled(total, a, gr[k1])
                total = add_scaled(total, b, gi[k1])
            out.append(total)
        return out

    def fwd_h(us, first):
        vs = [spin(u) for u in us]
        tu, tv = [], []
        for k1 in range(R):
            yu = yv = None
            for i in range(len(us)):
                a, b = root(R, (first + i) * k1)
                yu = add_scaled(add_scaled(yu, a, us[i]), b, vs[i])
                yv = add_scaled(add_scaled(yv, a, vs[i]), -b, us[i])
            ct, st = tw_h[:, k1:k1 + 1], tw_h[:, R + k1:R + k1 + 1]
            tu.append(yu * ct + yv * st)
            tv.append(yv * ct - yu * st)
        return dot(mat_h[0], jnp.concatenate(tu, 1)) + dot(mat_h[1], jnp.concatenate(tv, 1))

    def inv_h(ps, first, last):
        vs = [spin(p) for p in ps]
        g = (dot(mat_h[0], jnp.concatenate(ps, 1)) - dot(mat_h[1], jnp.concatenate(vs, 1))) * (1.0 / H)
        gu, gv = [], []
        for k1 in range(R):
            u = g[:, 2 * q * k1:2 * q * (k1 + 1)]
            v = spin(u)
            ct, st = tw_h[:, k1:k1 + 1], tw_h[:, R + k1:R + k1 + 1]
            gu.append(u * ct - v * st)
            gv.append(v * ct + u * st)
        out = []
        for n1 in range(first, last):
            total = None
            for k1 in range(R):
                a, b = root(R, n1 * k1)
                total = add_scaled(add_scaled(total, a, gu[k1]), -b, gv[k1])
            out.append(total)
        return out

    def kernel_parts(k1):
        k = jnp.concatenate([k_recv[j, k1 * t_rows:(k1 + 1) * t_rows, :] for j in range(R)], 0)
        rolled = pltpu.roll(k, q, 1)
        lane = lax.broadcasted_iota(jnp.int32, k.shape, 1)
        return jnp.where(lane < q, k, rolled), jnp.where(lane < q, rolled, k)

    x_vol.wait()
    z = fwd_w([r_vol[j] for j in range(C)], 0)
    for k1 in range(R):
        for j in range(C):
            s1[k1 * C + j] = z[k1 * rows:(k1 + 1) * rows, 2 * q * j:2 * q * (j + 1)]
    x1.start()
    x_k.start()
    r1[me16] = s1[me16]
    k_recv[r] = k_send[r]
    x1.wait()
    x_k.wait()

    def joined(ref, first, count):
        return jnp.concatenate([ref[first + j] for j in range(count)], 0)

    s = fwd_h([joined(r1, j * C, C) for j in range(R)], 0)
    ps = []
    for k1 in range(R):
        kr, ki = kernel_parts(k1)
        u = s[:, 2 * q * k1:2 * q * (k1 + 1)]
        ps.append(kr * u + ki * spin(u))
    xs = inv_h(ps, lo, hi)

    for i in range(NR):
        for j in range(C):
            for e in range(D):
                s2[(e * NR + i) * C + j] = xs[i][j * rows + e * rs:j * rows + (e + 1) * rs, :]

    def owner_id(t):
        return (t // (NR * C)) * n16 + (lo + (t // C) % NR) * C + t % C

    def send2(o):
        t = lax.rem(me + o, NO)
        w = owner_id(t)

        @pl.when(w != me)
        def _():
            rc(s2.at[t], r2.at[me], sm2s.at[t], sm2r.at[me], ids(w)).start()

        @pl.when(w == me)
        def _():
            r2[me] = s2[t]

    loop(0, NO, send2)
    x_meas.wait()
    is_owner = (r >= lo) & (r < hi)
    my_owner = ((r - lo) * C + c) * D + d

    @pl.when(is_owner)
    def _():
        def wait2(o):
            t = lax.rem(me + o, N)
            rc(r2.at[t], r2.at[t], sm2s.at[0], sm2r.at[t], ids(t)).wait_recv()

        loop(1, N, wait2)
        zs = []
        for k1 in range(R):
            pieces = []
            for j in range(C):
                total = r2[k1 * C + j]
                for e in range(1, D):
                    total = total + r2[e * n16 + k1 * C + j]
                pieces.append(total)
            zs.append(jnp.concatenate(pieces, 1))
        sensor = inv_w(jnp.concatenate(zs, 0), rs, lo_c, hi_c)
        res = [sensor[i] - r_meas[lo_c + i] for i in range(hi_c - lo_c)]
        zz = fwd_w(res, lo_c)
        for k1 in range(R):
            for j in range(C):
                s3[k1 * C + j] = zz[k1 * rs:(k1 + 1) * rs, 2 * q * j:2 * q * (j + 1)]

        def send3(o):
            t = lax.rem(me + o, N)
            rc(s3.at[lax.rem(t, n16)], r3.at[my_owner], sm3s.at[t], sm3r.at[my_owner], ids(t)).start()

        loop(1, N, send3)
        r3[my_owner] = s3[me16]

        def drain3(o):
            t = lax.rem(me + o, N)
            rc(s3.at[lax.rem(t, n16)], r3.at[my_owner], sm3s.at[t], sm3r.at[my_owner], ids(t)).wait_send()

        loop(1, N, drain3)

    def drain2(o):
        t = lax.rem(me + o, NO)
        w = owner_id(t)

        @pl.when(w != me)
        def _():
            rc(s2.at[t], r2.at[me], sm2s.at[t], sm2r.at[me], ids(w)).wait_send()

    loop(0, NO, drain2)

    def wait3(t):
        w = (t % D) * n16 + (lo + t // (C * D)) * C + (t // D) % C

        @pl.when(w != me)
        def _():
            rc(r3.at[t], r3.at[t], sm3s.at[0], sm3r.at[t], ids(w)).wait_recv()

    loop(0, NO, wait3)
    s = fwd_h([joined(r3, i * C * D, C * D) for i in range(NR)], lo)
    ps = []
    for k1 in range(R):
        kr, ki = kernel_parts(k1)
        u = s[:, 2 * q * k1:2 * q * (k1 + 1)]
        ps.append(kr * u - ki * spin(u))
    xs = inv_h(ps, 0, R)
    for i in range(R):
        for j in range(C):
            s4[i * C + j] = xs[i][j * rows:(j + 1) * rows, :]
    x4.start()
    r4[me16] = s4[me16]
    x4.wait()
    zs = [jnp.concatenate([r4[k1 * C + j] for j in range(C)], 1) for k1 in range(R)]
    adj = inv_w(jnp.concatenate(zs, 0), rows, 0, C)
    for j in range(C):
        s5[j] = adj[j]
    x5.start()
    r5[c] = s5[c]
    x5.wait()
    for j in range(C):
        ups[j * rows:(j + 1) * rows, :] = vol[j] - step_size * r5[j]

    down_d, down_r, down_c = lax.rem(d + D - 1, D), lax.rem(r + R - 1, R), lax.rem(c + C - 1, C)
    copies = [
        rc(ups.at[0:8, :], h_row, sm_h.at[0, 1], sm_h.at[1, 1], {"row": down_r}),
        rc(ups.at[:, 0:128], h_col, sm_h.at[0, 2], sm_h.at[1, 2], {"col": down_c}),
        rc(ups, h_dep, sm_h.at[0, 0], sm_h.at[1, 0], {"depth": down_d}),
    ]
    for cp in copies:
        cp.start()
    u = ups[...]
    upd[0] = u

    def finish(i, diff):
        combined = diff + dual[i, 0]
        clipped = jnp.clip(combined, -shrink_level, shrink_level)
        shr[i, 0] = combined - clipped
        dnx[i, 0] = clipped

    copies[0].wait()
    rid = lax.broadcasted_iota(jnp.int32, (hb, wb), 0)
    nxt = jnp.where(rid == hb - 1, jnp.broadcast_to(h_row[0:1, :], (hb, wb)), pltpu.roll(u, hb - 1, 0))
    finish(1, jnp.where(r * hb + rid < H - 1, nxt - u, 0.0))
    copies[1].wait()
    cid = lax.broadcasted_iota(jnp.int32, (hb, wb), 1)
    nxt = jnp.where(cid == wb - 1, jnp.broadcast_to(h_col[:, 0:1], (hb, wb)), pltpu.roll(u, wb - 1, 1))
    finish(2, jnp.where(c * wb + cid < W - 1, nxt - u, 0.0))
    copies[2].wait()
    live = (d + rid * 0) < D - 1
    finish(0, jnp.where(live, h_dep[...] - u, 0.0))


def shards(D, R, C, volume, psf_spec, measured, dual):
    planes, hb, wb = volume.shape
    assert planes == 1 and R == C
    H, W = hb * R, wb * C
    rows, q = hb // C, wb // R
    rs = rows // D
    NO, N, n16 = D * (3 * R // 4 - R // 4) * C, D * R * C, R * C
    n2, k2 = np.arange(wb), np.arange(wb)
    f = np.exp(-2j * np.pi * ((n2[:, None] * k2[None]) % wb) / wb).reshape(wb, C, 1, wb // C)
    top = np.concatenate([f.real, f.imag], 2).reshape(wb, 2 * wb)
    bot = np.concatenate([-f.imag, f.real], 2).reshape(wb, 2 * wb)
    mat_w = np.concatenate([top, bot], 0).astype(np.float32)
    m = np.arange(hb)
    g = np.exp(-2j * np.pi * ((m[:, None] * m[None]) % hb) / hb)
    mat_h = np.stack([g.real, g.imag]).astype(np.float32)
    t = np.exp(-2j * np.pi * (np.arange(C)[:, None] * n2[None]) / W)
    tw_w = np.stack([t.real, t.imag]).astype(np.float32)
    t = np.exp(-2j * np.pi * (m[:, None] * np.arange(R)[None]) / H)
    tw_h = np.concatenate([t.real, t.imag], 1).astype(np.float32)
    f32 = jnp.float32
    V = pltpu.VMEM
    dma = pltpu.SemaphoreType.DMA
    vm = pl.BlockSpec(memory_space=pltpu.VMEM)
    return pl.pallas_call(
        functools.partial(body, D, R, C, hb, wb),
        name="admm",
        out_shape=(
            jax.ShapeDtypeStruct((1, hb, wb), f32),
            jax.ShapeDtypeStruct((3, 1, hb, wb), f32),
            jax.ShapeDtypeStruct((3, 1, hb, wb), f32),
        ),
        in_specs=[vm] * 8,
        out_specs=(vm, vm, vm),
        scratch_shapes=[
            V((C, rows, wb), f32),
            V((R, hb, 2 * q), f32), V((R, hb, 2 * q), f32),
            V((C, rs, wb), f32),
            V((n16, rows, 2 * q), f32), V((n16, rows, 2 * q), f32),
            V((NO, rs, 2 * q), f32), V((N, rs, 2 * q), f32),
            V((n16, rs, 2 * q), f32), V((NO, rs, 2 * q), f32),
            V((n16, rows, 2 * q), f32), V((n16, rows, 2 * q), f32),
            V((C, rows, wb), f32), V((C, rows, wb), f32),
            V((hb, wb), f32), V((hb, wb), f32), V((8, wb), f32), V((hb, 128), f32),
            dma((2, C)), dma((2, R)), dma((2, C)), dma((2, n16)), dma((NO,)), dma((N,)),
            dma((N,)), dma((NO,)), dma((2, n16)), dma((2, C)), dma((2, 3)),
        ],
        compiler_params=pltpu.CompilerParams(
            collective_id=0, has_side_effects=True, vmem_limit_bytes=60 * 1024 * 1024
        ),
    )(
        volume.reshape(C, rows, wb), psf_spec.reshape(2, hb, wb), measured.reshape(C, D, rs, wb), dual,
        jnp.asarray(mat_w), jnp.asarray(mat_h), jnp.asarray(tw_w), jnp.asarray(tw_h),
    )


def solution(mesh):
    placed = (
        P("depth", "row", "col"),
        P(None, "depth", "row", "col"),
        P("row", "col"),
        P(None, "depth", "row", "col"),
    )
    return jax.shard_map(
        functools.partial(shards, mesh.shape["depth"], mesh.shape["row"], mesh.shape["col"]),
        mesh=mesh,
        in_specs=placed,
        out_specs=(
            P("depth", "row", "col"),
            P(None, "depth", "row", "col"),
            P(None, "depth", "row", "col"),
        ),
        check_vma=False,
    )
```

```python
import functools

import jax
import jax.numpy as jnp
import numpy as np
from jax import lax
from jax.experimental import pallas as pl
from jax.experimental.pallas import tpu as pltpu
from jax.sharding import PartitionSpec as P

step_size = 1.0
shrink_level = 0.5
MESH = pl.DeviceIdType.MESH


def dot_of(a, b, side):
    return lax.dot_general(a, b, (((1,), (side,)), ((), ())), preferred_element_type=jnp.float32)


def halves(a):
    high = a.astype(jnp.bfloat16)
    return high, (a - high.astype(jnp.float32)).astype(jnp.bfloat16)


def dot_right(a, table, side):
    high, low = halves(a)
    return dot_of(high, table[0], side) + (dot_of(high, table[1], side) + dot_of(low, table[0], side))


def dot_left(table, b):
    high, low = b
    return dot_of(table[0], high, 0) + (dot_of(table[0], low, 0) + dot_of(table[1], high, 0))


def root(count, n):
    value = np.exp(-2j * np.pi * (n % count) / count)
    real, imag = float(value.real), float(value.imag)
    real = round(real) if abs(real - round(real)) < 1e-12 else real
    imag = round(imag) if abs(imag - round(imag)) < 1e-12 else imag
    return float(real), float(imag)


def add_scaled(total, scale, value):
    if scale == 0.0:
        return total
    if total is None:
        return value if scale == 1.0 else (-value if scale == -1.0 else scale * value)
    if scale == 1.0:
        return total + value
    if scale == -1.0:
        return total - value
    return total + scale * value


def spin(u):
    half = u.shape[-1] // 2
    lane = lax.broadcasted_iota(jnp.int32, u.shape, u.ndim - 1)
    rolled = pltpu.roll(u, half, u.ndim - 1)
    return jnp.where(lane < half, -rolled, rolled)


def body(D, R, C, hb, wb,
         vol, psf, meas, mat_w, mat_h, tw_w, tw_h,
         out_u, out_dep, out_row, out_col,
         r_vol, k_send, k_recv, r_meas, s1, r1, s2, r2, s3, r3, s4, r4, s5, r5, ups, h_dep, h_row, h_col, edge,
         sm_vol, sm_k, sm_meas, sm1, sm2s, sm2r, sm3s, sm3r, sm4, sm5, sm_h, sm_dep):
    H, W = R * hb, C * wb
    rows, q = hb // C, wb // R
    rs = rows // D
    lo, hi, lo_c, hi_c = R // 4, 3 * R // 4, C // 4, 3 * C // 4
    NR = hi - lo
    N, n16, NO = D * R * C, R * C, D * NR * C
    d, r, c = lax.axis_index("depth"), lax.axis_index("row"), lax.axis_index("col")
    me16 = r * C + c
    me = d * n16 + me16

    def ids(t):
        return {"depth": t // n16, "row": (t // C) % R, "col": t % C}

    barrier = pltpu.get_barrier_semaphore()

    def greet(o, _):
        pl.semaphore_signal(barrier, inc=1, device_id=ids(lax.rem(me + o, N)), device_id_type=MESH)
        return 0

    lax.fori_loop(1, N, greet, 0)

    def rc(src, dst, ss, rsm, dev):
        return pltpu.make_async_remote_copy(src_ref=src, dst_ref=dst, send_sem=ss, recv_sem=rsm, device_id=dev, device_id_type=MESH)

    def loop(lower, upper, f):
        def g(i, x):
            f(i)
            return x
        lax.fori_loop(lower, upper, g, 0)

    class A2A:
        def __init__(self, n, pos, dev, src, recv, sems):
            self.n, self.pos, self.dev, self.src, self.recv, self.sems = n, pos, dev, src, recv, sems

        def start(self):
            def go(o):
                t = lax.rem(self.pos + o, self.n)
                rc(self.src(t), self.recv.at[self.pos], self.sems.at[0, t], self.sems.at[1, self.pos], self.dev(t)).start()
            loop(1, self.n, go)

        def wait(self):
            def go(o):
                t = lax.rem(self.pos + o, self.n)
                rc(self.src(t), self.recv.at[t], self.sems.at[0, t], self.sems.at[1, t], self.dev(t)).wait()
            loop(1, self.n, go)

    col_dev = lambda t: {"col": t}
    row_dev = lambda t: {"row": t}
    all_dev = lambda t: {"row": t // C, "col": lax.rem(t, C)}

    x_vol = A2A(C, c, col_dev, lambda t: vol.at[t], r_vol, sm_vol)
    x_k = A2A(R, r, row_dev, lambda t: k_send.at[t], k_recv, sm_k)
    x_meas = A2A(C, c, col_dev, lambda t: meas.at[t, d], r_meas, sm_meas)
    x1 = A2A(n16, me16, all_dev, lambda t: s1.at[t], r1, sm1)
    x4 = A2A(n16, me16, all_dev, lambda t: s4.at[t], r4, sm4)
    x5 = A2A(C, c, col_dev, lambda t: s5.at[t], r5, sm5)

    pl.semaphore_wait(barrier, N - 1)
    x_vol.start()
    r_vol[c] = vol[c]

    kin = jnp.concatenate([psf[0], psf[1]], axis=1)
    i0 = lax.broadcasted_iota(jnp.int32, (2 * wb, 2 * wb), 0)
    i1 = lax.broadcasted_iota(jnp.int32, (2 * wb, 2 * wb), 1)
    target = (lax.rem(i1, 2 * q) // q) * wb + R * lax.rem(i1, q) + i1 // (2 * q)
    perm_c = jnp.where(i0 == target, 1.0, 0.0).astype(jnp.float32)
    j0 = lax.broadcasted_iota(jnp.int32, (hb, hb), 0)
    j1 = lax.broadcasted_iota(jnp.int32, (hb, hb), 1)
    t_rows = hb // R
    perm_r = jnp.where(j1 == R * lax.rem(j0, t_rows) + j0 // t_rows, 1.0, 0.0).astype(jnp.float32)
    perm_c, perm_r = perm_c.astype(jnp.bfloat16), perm_r.astype(jnp.bfloat16)
    kin_high, kin_low = halves(kin)
    kk = (dot_of(perm_r, dot_of(kin_high, perm_c, 0).astype(jnp.bfloat16), 0)
          + dot_of(perm_r, dot_of(kin_low, perm_c, 0).astype(jnp.bfloat16), 0))
    for j in range(R):
        k_send[j] = kk[:, 2 * q * j:2 * q * (j + 1)]
    x_k.start()
    k_recv[r] = k_send[r]
    x_meas.start()
    r_meas[c] = meas[c, d]

    def fwd_w(blocks, first):
        tre, tim = [], []
        for k1 in range(C):
            yr = yi = None
            for i, blk in enumerate(blocks):
                a, b = root(C, (first + i) * k1)
                yr, yi = add_scaled(yr, a, blk), add_scaled(yi, b, blk)
            ct, st = tw_w[0, k1:k1 + 1, :], tw_w[1, k1:k1 + 1, :]
            if yi is None:
                tre.append(yr * ct)
                tim.append(yr * st)
            else:
                tre.append(yr * ct - yi * st)
                tim.append(yr * st + yi * ct)
        both = jnp.concatenate([jnp.concatenate(tre, 0), jnp.concatenate(tim, 0)], 1)
        return dot_right(both, (mat_w[0], mat_w[1]), 0)

    def inv_w(z, count, first, last):
        g = dot_right(z, (mat_w[0], mat_w[1]), 1) * (1.0 / W)
        gr, gi = [], []
        for k1 in range(C):
            a = g[k1 * count:(k1 + 1) * count, :wb]
            b = g[k1 * count:(k1 + 1) * count, wb:]
            ct, st = tw_w[0, k1:k1 + 1, :], tw_w[1, k1:k1 + 1, :]
            gr.append(a * ct + b * st)
            gi.append(b * ct - a * st)
        out = []
        for n1 in range(first, last):
            total = None
            for k1 in range(C):
                a, b = root(C, n1 * k1)
                total = add_scaled(total, a, gr[k1])
                total = add_scaled(total, b, gi[k1])
            out.append(total)
        return out

    def fwd_h(us, first):
        vs = [spin(u) for u in us]
        tu, tv = [], []
        for k1 in range(R):
            yu = yv = None
            for i in range(len(us)):
                a, b = root(R, (first + i) * k1)
                yu = add_scaled(add_scaled(yu, a, us[i]), b, vs[i])
                yv = add_scaled(add_scaled(yv, a, vs[i]), -b, us[i])
            ct, st = tw_h[:, k1:k1 + 1], tw_h[:, R + k1:R + k1 + 1]
            tu.append(yu * ct + yv * st)
            tv.append(yv * ct - yu * st)
        return (dot_left((mat_h[0, 0], mat_h[1, 0]), halves(jnp.concatenate(tu, 1)))
                + dot_left((mat_h[0, 1], mat_h[1, 1]), halves(jnp.concatenate(tv, 1))))

    def inv_h(ps, first, last):
        vs = [spin(p) for p in ps]
        g = (dot_left((mat_h[0, 0], mat_h[1, 0]), halves(jnp.concatenate(ps, 1)))
             - dot_left((mat_h[0, 1], mat_h[1, 1]), halves(jnp.concatenate(vs, 1)))) * (1.0 / H)
        gu, gv = [], []
        for k1 in range(R):
            u = g[:, 2 * q * k1:2 * q * (k1 + 1)]
            v = spin(u)
            ct, st = tw_h[:, k1:k1 + 1], tw_h[:, R + k1:R + k1 + 1]
            gu.append(u * ct - v * st)
            gv.append(v * ct + u * st)
        out = []
        for n1 in range(first, last):
            total = None
            for k1 in range(R):
                a, b = root(R, n1 * k1)
                total = add_scaled(add_scaled(total, a, gu[k1]), -b, gv[k1])
            out.append(total)
        return out

    def kernel_parts(k1):
        k = jnp.concatenate([k_recv[j, k1 * t_rows:(k1 + 1) * t_rows, :] for j in range(R)], 0)
        rolled = pltpu.roll(k, q, 1)
        lane = lax.broadcasted_iota(jnp.int32, k.shape, 1)
        return jnp.where(lane < q, k, rolled), jnp.where(lane < q, rolled, k)

    x_vol.wait()
    z = fwd_w([r_vol[j] for j in range(C)], 0)
    for k1 in range(R):
        for j in range(C):
            s1[k1 * C + j] = z[k1 * rows:(k1 + 1) * rows, 2 * q * j:2 * q * (j + 1)]
    x1.start()
    r1[me16] = s1[me16]
    x1.wait()
    x_k.wait()

    def joined(ref, first, count):
        return jnp.concatenate([ref[first + j] for j in range(count)], 0)

    s = fwd_h([joined(r1, j * C, C) for j in range(R)], 0)
    ps = []
    for k1 in range(R):
        kr, ki = kernel_parts(k1)
        u = s[:, 2 * q * k1:2 * q * (k1 + 1)]
        ps.append(kr * u + ki * spin(u))
    xs = inv_h(ps, lo, hi)

    for i in range(NR):
        for j in range(C):
            for e in range(D):
                s2[(e * NR + i) * C + j] = xs[i][j * rows + e * rs:j * rows + (e + 1) * rs, :]

    def owner_id(t):
        return (t // (NR * C)) * n16 + (lo + (t // C) % NR) * C + t % C

    def send2(o):
        t = lax.rem(me + o, NO)
        w = owner_id(t)

        @pl.when(w != me)
        def _():
            rc(s2.at[t], r2.at[me], sm2s.at[t], sm2r.at[me], ids(w)).start()

        @pl.when(w == me)
        def _():
            r2[me] = s2[t]

    loop(0, NO, send2)
    x_meas.wait()
    is_owner = (r >= lo) & (r < hi)
    my_owner = ((r - lo) * C + c) * D + d

    @pl.when(is_owner)
    def _():
        def wait2(o):
            t = lax.rem(me + o, N)
            rc(r2.at[t], r2.at[t], sm2s.at[0], sm2r.at[t], ids(t)).wait_recv()

        loop(1, N, wait2)
        zs = []
        for k1 in range(R):
            pieces = []
            for j in range(C):
                total = r2[k1 * C + j]
                for e in range(1, D):
                    total = total + r2[e * n16 + k1 * C + j]
                pieces.append(total)
            zs.append(jnp.concatenate(pieces, 1))
        sensor = inv_w(jnp.concatenate(zs, 0), rs, lo_c, hi_c)
        res = [sensor[i] - r_meas[lo_c + i] for i in range(hi_c - lo_c)]
        zz = fwd_w(res, lo_c)
        for k1 in range(R):
            for j in range(C):
                s3[k1 * C + j] = zz[k1 * rs:(k1 + 1) * rs, 2 * q * j:2 * q * (j + 1)]

        def send3(o):
            t = lax.rem(me + o, N)
            rc(s3.at[lax.rem(t, n16)], r3.at[my_owner], sm3s.at[t], sm3r.at[my_owner], ids(t)).start()

        loop(1, N, send3)
        r3[my_owner] = s3[me16]

        def drain3(o):
            t = lax.rem(me + o, N)
            rc(s3.at[lax.rem(t, n16)], r3.at[my_owner], sm3s.at[t], sm3r.at[my_owner], ids(t)).wait_send()

        loop(1, N, drain3)

    def drain2(o):
        t = lax.rem(me + o, NO)
        w = owner_id(t)

        @pl.when(w != me)
        def _():
            rc(s2.at[t], r2.at[me], sm2s.at[t], sm2r.at[me], ids(w)).wait_send()

    loop(0, NO, drain2)

    def wait3(t):
        w = (t % D) * n16 + (lo + t // (C * D)) * C + (t // D) % C

        @pl.when(w != me)
        def _():
            rc(r3.at[t], r3.at[t], sm3s.at[0], sm3r.at[t], ids(w)).wait_recv()

    loop(0, NO, wait3)
    s = fwd_h([joined(r3, i * C * D, C * D) for i in range(NR)], lo)
    ps = []
    for k1 in range(R):
        kr, ki = kernel_parts(k1)
        u = s[:, 2 * q * k1:2 * q * (k1 + 1)]
        ps.append(kr * u - ki * spin(u))
    xs = inv_h(ps, 0, R)
    for i in range(R):
        for j in range(C):
            s4[i * C + j] = xs[i][j * rows:(j + 1) * rows, :]
    x4.start()
    r4[me16] = s4[me16]
    x4.wait()
    zs = [jnp.concatenate([r4[k1 * C + j] for j in range(C)], 1) for k1 in range(R)]
    adj = inv_w(jnp.concatenate(zs, 0), rows, 0, C)
    for j in range(C):
        s5[j] = adj[j]
    x5.start()
    down_d, down_r, down_c = lax.rem(d + D - 1, D), lax.rem(r + R - 1, R), lax.rem(c + C - 1, C)
    far = d > 0

    def plane_copy(t):
        return rc(ups.at[t], h_dep.at[t], sm_dep.at[0, t], sm_dep.at[1, t], {"depth": d - 1})

    def take(t, value):
        ups[t] = vol[t] - step_size * value

        @pl.when(far)
        def _():
            plane_copy(t).start()

    take(c, s5[c])

    def arrive(o):
        t = lax.rem(c + o, C)
        rc(s5.at[t], r5.at[t], sm5.at[0, t], sm5.at[1, t], col_dev(t)).wait()
        take(t, r5[t])

    loop(1, C, arrive)
    for j in range(C):
        edge[j * rows:(j + 1) * rows, :] = ups[j, :, 0:128]
    copies = [
        rc(ups.at[0, 0:8, :], h_row, sm_h.at[0, 0], sm_h.at[1, 0], {"row": down_r}),
        rc(edge, h_col, sm_h.at[0, 1], sm_h.at[1, 1], {"col": down_c}),
    ]
    for cp in copies:
        cp.start()
    for j in range(C):
        out_u[j * rows:(j + 1) * rows, :] = ups[j]
    copies[0].wait()
    out_row[...] = h_row[...]
    copies[1].wait()
    out_col[...] = h_col[...]

    @pl.when(far)
    def _():
        def sent(t):
            plane_copy(t).wait_send()

        loop(0, C, sent)

    @pl.when(d < D - 1)
    def _():
        def landed(t):
            rc(ups.at[t], h_dep.at[t], sm_dep.at[0, t], sm_dep.at[1, t], {"depth": d + 1}).wait_recv()

        loop(0, C, landed)
        for j in range(C):
            out_dep[j * rows:(j + 1) * rows, :] = h_dep[j]

    @pl.when(d == D - 1)
    def _():
        for j in range(C):
            out_dep[j * rows:(j + 1) * rows, :] = ups[j]


def tail(D, R, C, ups, dep, row, col, dual, upd, shr, dnx):
    hb, wb = ups.shape
    r, c = lax.axis_index("row"), lax.axis_index("col")
    u = ups[...]
    upd[0] = u

    def finish(i, diff):
        combined = diff + dual[i, 0]
        clipped = jnp.clip(combined, -shrink_level, shrink_level)
        shr[i, 0] = combined - clipped
        dnx[i, 0] = clipped

    finish(0, dep[...] - u)
    rid = lax.broadcasted_iota(jnp.int32, (hb, wb), 0)
    nxt = jnp.where(rid == hb - 1, jnp.broadcast_to(row[0:1, :], (hb, wb)), pltpu.roll(u, hb - 1, 0))
    finish(1, jnp.where(r * hb + rid < hb * R - 1, nxt - u, 0.0))
    cid = lax.broadcasted_iota(jnp.int32, (hb, wb), 1)
    nxt = jnp.where(cid == wb - 1, jnp.broadcast_to(col[:, 0:1], (hb, wb)), pltpu.roll(u, wb - 1, 1))
    finish(2, jnp.where(c * wb + cid < wb * C - 1, nxt - u, 0.0))


def two_halves(table):
    high = table.astype(jnp.bfloat16)
    return np.stack([high, (table - high.astype(np.float64)).astype(jnp.bfloat16)])


def shards(D, R, C, volume, psf_spec, measured, dual):
    planes, hb, wb = volume.shape
    assert planes == 1 and R == C
    H, W = hb * R, wb * C
    rows, q = hb // C, wb // R
    rs = rows // D
    NO, N, n16 = D * (3 * R // 4 - R // 4) * C, D * R * C, R * C
    n2, k2 = np.arange(wb), np.arange(wb)
    f = np.exp(-2j * np.pi * ((n2[:, None] * k2[None]) % wb) / wb).reshape(wb, C, 1, wb // C)
    top = np.concatenate([f.real, f.imag], 2).reshape(wb, 2 * wb)
    bot = np.concatenate([-f.imag, f.real], 2).reshape(wb, 2 * wb)
    mat_w = two_halves(np.concatenate([top, bot], 0))
    m = np.arange(hb)
    g = np.exp(-2j * np.pi * ((m[:, None] * m[None]) % hb) / hb)
    mat_h = two_halves(np.stack([g.real, g.imag]))
    t = np.exp(-2j * np.pi * (np.arange(C)[:, None] * n2[None]) / W)
    tw_w = np.stack([t.real, t.imag]).astype(np.float32)
    t = np.exp(-2j * np.pi * (m[:, None] * np.arange(R)[None]) / H)
    tw_h = np.concatenate([t.real, t.imag], 1).astype(np.float32)
    f32 = jnp.float32
    V = pltpu.VMEM
    dma = pltpu.SemaphoreType.DMA
    vm = pl.BlockSpec(memory_space=pltpu.VMEM)
    near = pl.pallas_call(
        functools.partial(body, D, R, C, hb, wb),
        name="admm",
        out_shape=(
            jax.ShapeDtypeStruct((hb, wb), f32),
            jax.ShapeDtypeStruct((hb, wb), f32),
            jax.ShapeDtypeStruct((8, wb), f32),
            jax.ShapeDtypeStruct((hb, 128), f32),
        ),
        in_specs=[vm] * 7,
        out_specs=(vm, vm, vm, vm),
        scratch_shapes=[
            V((C, rows, wb), f32),
            V((R, hb, 2 * q), f32), V((R, hb, 2 * q), f32),
            V((C, rs, wb), f32),
            V((n16, rows, 2 * q), f32), V((n16, rows, 2 * q), f32),
            V((NO, rs, 2 * q), f32), V((N, rs, 2 * q), f32),
            V((n16, rs, 2 * q), f32), V((NO, rs, 2 * q), f32),
            V((n16, rows, 2 * q), f32), V((n16, rows, 2 * q), f32),
            V((C, rows, wb), f32), V((C, rows, wb), f32),
            V((C, rows, wb), f32), V((C, rows, wb), f32), V((8, wb), f32), V((hb, 128), f32), V((hb, 128), f32),
            dma((2, C)), dma((2, R)), dma((2, C)), dma((2, n16)), dma((NO,)), dma((N,)),
            dma((N,)), dma((NO,)), dma((2, n16)), dma((2, C)), dma((2, 2)), dma((2, C)),
        ],
        compiler_params=pltpu.CompilerParams(
            collective_id=0, has_side_effects=True, vmem_limit_bytes=60 * 1024 * 1024
        ),
    )(
        volume.reshape(C, rows, wb), psf_spec.reshape(2, hb, wb), measured.reshape(C, D, rs, wb),
        jnp.asarray(mat_w), jnp.asarray(mat_h), jnp.asarray(tw_w), jnp.asarray(tw_h),
    )
    return pl.pallas_call(
        functools.partial(tail, D, R, C),
        name="tail",
        out_shape=(
            jax.ShapeDtypeStruct((1, hb, wb), f32),
            jax.ShapeDtypeStruct((3, 1, hb, wb), f32),
            jax.ShapeDtypeStruct((3, 1, hb, wb), f32),
        ),
        in_specs=[vm] * 5,
        out_specs=(vm, vm, vm),
        compiler_params=pltpu.CompilerParams(vmem_limit_bytes=16 * 1024 * 1024),
    )(*near, dual)


def solution(mesh):
    placed = (
        P("depth", "row", "col"),
        P(None, "depth", "row", "col"),
        P("row", "col"),
        P(None, "depth", "row", "col"),
    )
    return jax.shard_map(
        functools.partial(shards, mesh.shape["depth"], mesh.shape["row"], mesh.shape["col"]),
        mesh=mesh,
        in_specs=placed,
        out_specs=(
            P("depth", "row", "col"),
            P(None, "depth", "row", "col"),
            P(None, "depth", "row", "col"),
        ),
        check_vma=False,
    )
```

```python
import functools

import jax
import jax.numpy as jnp
import numpy as np
from jax import lax
from jax.experimental import pallas as pl
from jax.experimental.pallas import tpu as pltpu
from jax.sharding import PartitionSpec as P

step_size = 1.0
shrink_level = 0.5
MESH = pl.DeviceIdType.MESH


def dot_of(a, b, side):
    return lax.dot_general(a, b, (((1,), (side,)), ((), ())), preferred_element_type=jnp.float32)


def halves(a):
    high = a.astype(jnp.bfloat16)
    return high, (a - high.astype(jnp.float32)).astype(jnp.bfloat16)


def dot_right(a, table, side):
    high, low = halves(a)
    return dot_of(high, table[0], side) + (dot_of(high, table[1], side) + dot_of(low, table[0], side))


def dot_left(table, b):
    high, low = b
    return dot_of(table[0], high, 0) + (dot_of(table[0], low, 0) + dot_of(table[1], high, 0))


def root(count, n):
    value = np.exp(-2j * np.pi * (n % count) / count)
    real, imag = float(value.real), float(value.imag)
    real = round(real) if abs(real - round(real)) < 1e-12 else real
    imag = round(imag) if abs(imag - round(imag)) < 1e-12 else imag
    return float(real), float(imag)


def add_scaled(total, scale, value):
    if scale == 0.0:
        return total
    if total is None:
        return value if scale == 1.0 else (-value if scale == -1.0 else scale * value)
    if scale == 1.0:
        return total + value
    if scale == -1.0:
        return total - value
    return total + scale * value


def spin(u):
    half = u.shape[-1] // 2
    lane = lax.broadcasted_iota(jnp.int32, u.shape, u.ndim - 1)
    rolled = pltpu.roll(u, half, u.ndim - 1)
    return jnp.where(lane < half, -rolled, rolled)


def body(D, R, C, hb, wb,
         vol, psf, meas, mat_w, mat_h, tw_w, tw_h,
         out_u, out_dep, out_row, out_col,
         r_vol, k_send, k_recv, r_meas, s1, r1, s2, r2, s3, r3, s4, r4, s5, r5, ups, h_dep, h_row, h_col, edge,
         sm_vol, sm_k, sm_meas, sm1, sm2s, sm2r, sm3s, sm3r, sm4, sm5, sm_h, sm_dep):
    H, W = R * hb, C * wb
    rows, q = hb // C, wb // R
    rs = rows // D
    lo, hi, lo_c, hi_c = R // 4, 3 * R // 4, C // 4, 3 * C // 4
    NR = hi - lo
    N, n16, NO = D * R * C, R * C, D * NR * C
    d, r, c = lax.axis_index("depth"), lax.axis_index("row"), lax.axis_index("col")
    me16 = r * C + c
    me = d * n16 + me16

    def ids(t):
        return {"depth": t // n16, "row": (t // C) % R, "col": t % C}

    barrier = pltpu.get_barrier_semaphore()

    def greet(o, _):
        pl.semaphore_signal(barrier, inc=1, device_id=ids(lax.rem(me + o, N)), device_id_type=MESH)
        return 0

    lax.fori_loop(1, N, greet, 0)

    def rc(src, dst, ss, rsm, dev):
        return pltpu.make_async_remote_copy(src_ref=src, dst_ref=dst, send_sem=ss, recv_sem=rsm, device_id=dev, device_id_type=MESH)

    def loop(lower, upper, f):
        def g(i, x):
            f(i)
            return x
        lax.fori_loop(lower, upper, g, 0)

    class A2A:
        def __init__(self, n, pos, dev, src, recv, sems):
            self.n, self.pos, self.dev, self.src, self.recv, self.sems = n, pos, dev, src, recv, sems

        def start(self):
            def go(o):
                t = lax.rem(self.pos + o, self.n)
                rc(self.src(t), self.recv(self.pos), self.sems.at[0, t], self.sems.at[1, self.pos], self.dev(t)).start()
            loop(1, self.n, go)

        def wait(self):
            def go(o):
                t = lax.rem(self.pos + o, self.n)
                rc(self.src(t), self.recv(t), self.sems.at[0, t], self.sems.at[1, t], self.dev(t)).wait()
            loop(1, self.n, go)

    col_dev = lambda t: {"col": t}
    row_dev = lambda t: {"row": t}
    all_dev = lambda t: {"row": t // C, "col": lax.rem(t, C)}

    half = rows // 2

    def in_halves(n, pos, dev, send, recv, sems):
        def one(h):
            part = slice(h * half, (h + 1) * half)
            return A2A(n, pos, dev, lambda t: send.at[t, part], lambda t: recv.at[t, part], sems.at[h])
        return [one(0), one(1)]

    x_vol = in_halves(C, c, col_dev, vol, r_vol, sm_vol)
    x_k = A2A(R, r, row_dev, lambda t: k_send.at[t], lambda t: k_recv.at[t], sm_k)
    x_meas = A2A(C, c, col_dev, lambda t: meas.at[t, d], lambda t: r_meas.at[t], sm_meas)
    x1 = in_halves(n16, me16, all_dev, s1, r1, sm1)
    x4 = in_halves(n16, me16, all_dev, s4, r4, sm4)
    x5 = in_halves(C, c, col_dev, s5, r5, sm5)

    pl.semaphore_wait(barrier, N - 1)
    x_vol[0].start()
    x_vol[1].start()
    r_vol[c] = vol[c]

    kin = jnp.concatenate([psf[0], psf[1]], axis=1)
    i0 = lax.broadcasted_iota(jnp.int32, (2 * wb, 2 * wb), 0)
    i1 = lax.broadcasted_iota(jnp.int32, (2 * wb, 2 * wb), 1)
    target = (lax.rem(i1, 2 * q) // q) * wb + R * lax.rem(i1, q) + i1 // (2 * q)
    perm_c = jnp.where(i0 == target, 1.0, 0.0).astype(jnp.float32)
    j0 = lax.broadcasted_iota(jnp.int32, (hb, hb), 0)
    j1 = lax.broadcasted_iota(jnp.int32, (hb, hb), 1)
    t_rows = hb // R
    perm_r = jnp.where(j1 == R * lax.rem(j0, t_rows) + j0 // t_rows, 1.0, 0.0).astype(jnp.float32)
    perm_c, perm_r = perm_c.astype(jnp.bfloat16), perm_r.astype(jnp.bfloat16)
    kin_high, kin_low = halves(kin)
    kk = (dot_of(perm_r, dot_of(kin_high, perm_c, 0).astype(jnp.bfloat16), 0)
          + dot_of(perm_r, dot_of(kin_low, perm_c, 0).astype(jnp.bfloat16), 0))
    for j in range(R):
        k_send[j] = kk[:, 2 * q * j:2 * q * (j + 1)]
    x_k.start()
    k_recv[r] = k_send[r]
    x_meas.start()
    r_meas[c] = meas[c, d]

    def fwd_w(blocks, first):
        tre, tim = [], []
        for k1 in range(C):
            yr = yi = None
            for i, blk in enumerate(blocks):
                a, b = root(C, (first + i) * k1)
                yr, yi = add_scaled(yr, a, blk), add_scaled(yi, b, blk)
            ct, st = tw_w[0, k1:k1 + 1, :], tw_w[1, k1:k1 + 1, :]
            if yi is None:
                tre.append(yr * ct)
                tim.append(yr * st)
            else:
                tre.append(yr * ct - yi * st)
                tim.append(yr * st + yi * ct)
        both = jnp.concatenate([jnp.concatenate(tre, 0), jnp.concatenate(tim, 0)], 1)
        return dot_right(both, (mat_w[0], mat_w[1]), 0)

    def inv_w(z, count, first, last):
        g = dot_right(z, (mat_w[0], mat_w[1]), 1) * (1.0 / W)
        gr, gi = [], []
        for k1 in range(C):
            a = g[k1 * count:(k1 + 1) * count, :wb]
            b = g[k1 * count:(k1 + 1) * count, wb:]
            ct, st = tw_w[0, k1:k1 + 1, :], tw_w[1, k1:k1 + 1, :]
            gr.append(a * ct + b * st)
            gi.append(b * ct - a * st)
        out = []
        for n1 in range(first, last):
            total = None
            for k1 in range(C):
                a, b = root(C, n1 * k1)
                total = add_scaled(total, a, gr[k1])
                total = add_scaled(total, b, gi[k1])
            out.append(total)
        return out

    def fwd_h(us, first):
        vs = [spin(u) for u in us]
        tu, tv = [], []
        for k1 in range(R):
            yu = yv = None
            for i in range(len(us)):
                a, b = root(R, (first + i) * k1)
                yu = add_scaled(add_scaled(yu, a, us[i]), b, vs[i])
                yv = add_scaled(add_scaled(yv, a, vs[i]), -b, us[i])
            ct, st = tw_h[:, k1:k1 + 1], tw_h[:, R + k1:R + k1 + 1]
            tu.append(yu * ct + yv * st)
            tv.append(yv * ct - yu * st)
        return (dot_left((mat_h[0, 0], mat_h[1, 0]), halves(jnp.concatenate(tu, 1)))
                + dot_left((mat_h[0, 1], mat_h[1, 1]), halves(jnp.concatenate(tv, 1))))

    def inv_h(ps, first, last):
        vs = [spin(p) for p in ps]
        g = (dot_left((mat_h[0, 0], mat_h[1, 0]), halves(jnp.concatenate(ps, 1)))
             - dot_left((mat_h[0, 1], mat_h[1, 1]), halves(jnp.concatenate(vs, 1)))) * (1.0 / H)
        gu, gv = [], []
        for k1 in range(R):
            u = g[:, 2 * q * k1:2 * q * (k1 + 1)]
            v = spin(u)
            ct, st = tw_h[:, k1:k1 + 1], tw_h[:, R + k1:R + k1 + 1]
            gu.append(u * ct - v * st)
            gv.append(v * ct + u * st)
        out = []
        for n1 in range(first, last):
            total = None
            for k1 in range(R):
                a, b = root(R, n1 * k1)
                total = add_scaled(add_scaled(total, a, gu[k1]), -b, gv[k1])
            out.append(total)
        return out

    def kernel_parts(k1):
        k = jnp.concatenate([k_recv[j, k1 * t_rows:(k1 + 1) * t_rows, :] for j in range(R)], 0)
        rolled = pltpu.roll(k, q, 1)
        lane = lax.broadcasted_iota(jnp.int32, k.shape, 1)
        return jnp.where(lane < q, k, rolled), jnp.where(lane < q, rolled, k)

    for h in range(2):
        part = slice(h * half, (h + 1) * half)
        x_vol[h].wait()
        z = fwd_w([r_vol[j, part] for j in range(C)], 0)
        for k1 in range(R):
            for j in range(C):
                s1[k1 * C + j, part] = z[k1 * half:(k1 + 1) * half, 2 * q * j:2 * q * (j + 1)]
        x1[h].start()
    r1[me16] = s1[me16]
    x1[0].wait()
    x1[1].wait()
    x_k.wait()

    def joined(ref, first, count):
        return jnp.concatenate([ref[first + j] for j in range(count)], 0)

    s = fwd_h([joined(r1, j * C, C) for j in range(R)], 0)
    ps = []
    for k1 in range(R):
        kr, ki = kernel_parts(k1)
        u = s[:, 2 * q * k1:2 * q * (k1 + 1)]
        ps.append(kr * u + ki * spin(u))
    xs = inv_h(ps, lo, hi)

    for i in range(NR):
        for j in range(C):
            for e in range(D):
                s2[(e * NR + i) * C + j] = xs[i][j * rows + e * rs:j * rows + (e + 1) * rs, :]

    def owner_id(t):
        return (t // (NR * C)) * n16 + (lo + (t // C) % NR) * C + t % C

    def send2(o):
        t = lax.rem(me + o, NO)
        w = owner_id(t)

        @pl.when(w != me)
        def _():
            rc(s2.at[t], r2.at[me], sm2s.at[t], sm2r.at[me], ids(w)).start()

        @pl.when(w == me)
        def _():
            r2[me] = s2[t]

    loop(0, NO, send2)
    x_meas.wait()
    is_owner = (r >= lo) & (r < hi)
    my_owner = ((r - lo) * C + c) * D + d

    @pl.when(is_owner)
    def _():
        def wait2(o):
            t = lax.rem(me + o, N)
            rc(r2.at[t], r2.at[t], sm2s.at[0], sm2r.at[t], ids(t)).wait_recv()

        loop(1, N, wait2)
        zs = []
        for k1 in range(R):
            pieces = []
            for j in range(C):
                total = r2[k1 * C + j]
                for e in range(1, D):
                    total = total + r2[e * n16 + k1 * C + j]
                pieces.append(total)
            zs.append(jnp.concatenate(pieces, 1))
        sensor = inv_w(jnp.concatenate(zs, 0), rs, lo_c, hi_c)
        res = [sensor[i] - r_meas[lo_c + i] for i in range(hi_c - lo_c)]
        zz = fwd_w(res, lo_c)
        for k1 in range(R):
            for j in range(C):
                s3[k1 * C + j] = zz[k1 * rs:(k1 + 1) * rs, 2 * q * j:2 * q * (j + 1)]

        def send3(o):
            t = lax.rem(me + o, N)
            rc(s3.at[lax.rem(t, n16)], r3.at[my_owner], sm3s.at[t], sm3r.at[my_owner], ids(t)).start()

        loop(1, N, send3)
        r3[my_owner] = s3[me16]

        def drain3(o):
            t = lax.rem(me + o, N)
            rc(s3.at[lax.rem(t, n16)], r3.at[my_owner], sm3s.at[t], sm3r.at[my_owner], ids(t)).wait_send()

        loop(1, N, drain3)

    def drain2(o):
        t = lax.rem(me + o, NO)
        w = owner_id(t)

        @pl.when(w != me)
        def _():
            rc(s2.at[t], r2.at[me], sm2s.at[t], sm2r.at[me], ids(w)).wait_send()

    loop(0, NO, drain2)

    def wait3(t):
        w = (t % D) * n16 + (lo + t // (C * D)) * C + (t // D) % C

        @pl.when(w != me)
        def _():
            rc(r3.at[t], r3.at[t], sm3s.at[0], sm3r.at[t], ids(w)).wait_recv()

    loop(0, NO, wait3)
    s = fwd_h([joined(r3, i * C * D, C * D) for i in range(NR)], lo)
    ps = []
    for k1 in range(R):
        kr, ki = kernel_parts(k1)
        u = s[:, 2 * q * k1:2 * q * (k1 + 1)]
        ps.append(kr * u - ki * spin(u))
    xs = inv_h(ps, 0, R)
    for i in range(R):
        for j in range(C):
            s4[i * C + j] = xs[i][j * rows:(j + 1) * rows, :]
    x4[0].start()
    x4[1].start()
    r4[me16] = s4[me16]
    for h in range(2):
        part = slice(h * half, (h + 1) * half)
        x4[h].wait()
        zs = [jnp.concatenate([r4[k1 * C + j, part] for j in range(C)], 1) for k1 in range(R)]
        adj = inv_w(jnp.concatenate(zs, 0), half, 0, C)
        for j in range(C):
            s5[j, part] = adj[j]
        x5[h].start()
    down_d, down_r, down_c = lax.rem(d + D - 1, D), lax.rem(r + R - 1, R), lax.rem(c + C - 1, C)
    far = d > 0

    def plane_copy(t, h, to):
        part = slice(h * half, (h + 1) * half)
        return rc(ups.at[t, part], h_dep.at[t, part], sm_dep.at[h, 0, t], sm_dep.at[h, 1, t], {"depth": to})

    for h in range(2):
        part = slice(h * half, (h + 1) * half)

        def take(t, value):
            ups[t, part] = vol[t, part] - step_size * value

            @pl.when(far)
            def _():
                plane_copy(t, h, d - 1).start()

        take(c, s5[c, part])

        def arrive(o):
            t = lax.rem(c + o, C)
            rc(s5.at[t, part], r5.at[t, part], sm5.at[h, 0, t], sm5.at[h, 1, t], col_dev(t)).wait()
            take(t, r5[t, part])

        loop(1, C, arrive)
    for j in range(C):
        edge[j * rows:(j + 1) * rows, :] = ups[j, :, 0:128]
    copies = [
        rc(ups.at[0, 0:8, :], h_row, sm_h.at[0, 0], sm_h.at[1, 0], {"row": down_r}),
        rc(edge, h_col, sm_h.at[0, 1], sm_h.at[1, 1], {"col": down_c}),
    ]
    for cp in copies:
        cp.start()
    for j in range(C):
        out_u[j * rows:(j + 1) * rows, :] = ups[j]
    copies[0].wait()
    out_row[...] = h_row[...]
    copies[1].wait()
    out_col[...] = h_col[...]

    @pl.when(far)
    def _():
        def sent(t):
            plane_copy(t, 0, d - 1).wait_send()
            plane_copy(t, 1, d - 1).wait_send()

        loop(0, C, sent)

    @pl.when(d < D - 1)
    def _():
        def landed(t):
            plane_copy(t, 0, d + 1).wait_recv()
            plane_copy(t, 1, d + 1).wait_recv()

        loop(0, C, landed)
        for j in range(C):
            out_dep[j * rows:(j + 1) * rows, :] = h_dep[j]

    @pl.when(d == D - 1)
    def _():
        for j in range(C):
            out_dep[j * rows:(j + 1) * rows, :] = ups[j]


def tail(D, R, C, ups, dep, row, col, dual, upd, shr, dnx):
    hb, wb = ups.shape
    r, c = lax.axis_index("row"), lax.axis_index("col")
    u = ups[...]
    upd[0] = u

    def finish(i, diff):
        combined = diff + dual[i, 0]
        clipped = jnp.clip(combined, -shrink_level, shrink_level)
        shr[i, 0] = combined - clipped
        dnx[i, 0] = clipped

    finish(0, dep[...] - u)
    rid = lax.broadcasted_iota(jnp.int32, (hb, wb), 0)
    nxt = jnp.where(rid == hb - 1, jnp.broadcast_to(row[0:1, :], (hb, wb)), pltpu.roll(u, hb - 1, 0))
    finish(1, jnp.where(r * hb + rid < hb * R - 1, nxt - u, 0.0))
    cid = lax.broadcasted_iota(jnp.int32, (hb, wb), 1)
    nxt = jnp.where(cid == wb - 1, jnp.broadcast_to(col[:, 0:1], (hb, wb)), pltpu.roll(u, wb - 1, 1))
    finish(2, jnp.where(c * wb + cid < wb * C - 1, nxt - u, 0.0))


def two_halves(table):
    high = table.astype(jnp.bfloat16)
    return np.stack([high, (table - high.astype(np.float64)).astype(jnp.bfloat16)])


def shards(D, R, C, volume, psf_spec, measured, dual):
    planes, hb, wb = volume.shape
    assert planes == 1 and R == C
    H, W = hb * R, wb * C
    rows, q = hb // C, wb // R
    rs = rows // D
    NO, N, n16 = D * (3 * R // 4 - R // 4) * C, D * R * C, R * C
    n2, k2 = np.arange(wb), np.arange(wb)
    f = np.exp(-2j * np.pi * ((n2[:, None] * k2[None]) % wb) / wb).reshape(wb, C, 1, wb // C)
    top = np.concatenate([f.real, f.imag], 2).reshape(wb, 2 * wb)
    bot = np.concatenate([-f.imag, f.real], 2).reshape(wb, 2 * wb)
    mat_w = two_halves(np.concatenate([top, bot], 0))
    m = np.arange(hb)
    g = np.exp(-2j * np.pi * ((m[:, None] * m[None]) % hb) / hb)
    mat_h = two_halves(np.stack([g.real, g.imag]))
    t = np.exp(-2j * np.pi * (np.arange(C)[:, None] * n2[None]) / W)
    tw_w = np.stack([t.real, t.imag]).astype(np.float32)
    t = np.exp(-2j * np.pi * (m[:, None] * np.arange(R)[None]) / H)
    tw_h = np.concatenate([t.real, t.imag], 1).astype(np.float32)
    f32 = jnp.float32
    V = pltpu.VMEM
    dma = pltpu.SemaphoreType.DMA
    vm = pl.BlockSpec(memory_space=pltpu.VMEM)
    near = pl.pallas_call(
        functools.partial(body, D, R, C, hb, wb),
        name="admm",
        out_shape=(
            jax.ShapeDtypeStruct((hb, wb), f32),
            jax.ShapeDtypeStruct((hb, wb), f32),
            jax.ShapeDtypeStruct((8, wb), f32),
            jax.ShapeDtypeStruct((hb, 128), f32),
        ),
        in_specs=[vm] * 7,
        out_specs=(vm, vm, vm, vm),
        scratch_shapes=[
            V((C, rows, wb), f32),
            V((R, hb, 2 * q), f32), V((R, hb, 2 * q), f32),
            V((C, rs, wb), f32),
            V((n16, rows, 2 * q), f32), V((n16, rows, 2 * q), f32),
            V((NO, rs, 2 * q), f32), V((N, rs, 2 * q), f32),
            V((n16, rs, 2 * q), f32), V((NO, rs, 2 * q), f32),
            V((n16, rows, 2 * q), f32), V((n16, rows, 2 * q), f32),
            V((C, rows, wb), f32), V((C, rows, wb), f32),
            V((C, rows, wb), f32), V((C, rows, wb), f32), V((8, wb), f32), V((hb, 128), f32), V((hb, 128), f32),
            dma((2, 2, C)), dma((2, R)), dma((2, C)), dma((2, 2, n16)), dma((NO,)), dma((N,)),
            dma((N,)), dma((NO,)), dma((2, 2, n16)), dma((2, 2, C)), dma((2, 2)), dma((2, 2, C)),
        ],
        compiler_params=pltpu.CompilerParams(
            collective_id=0, has_side_effects=True, vmem_limit_bytes=60 * 1024 * 1024
        ),
    )(
        volume.reshape(C, rows, wb), psf_spec.reshape(2, hb, wb), measured.reshape(C, D, rs, wb),
        jnp.asarray(mat_w), jnp.asarray(mat_h), jnp.asarray(tw_w), jnp.asarray(tw_h),
    )
    return pl.pallas_call(
        functools.partial(tail, D, R, C),
        name="tail",
        out_shape=(
            jax.ShapeDtypeStruct((1, hb, wb), f32),
            jax.ShapeDtypeStruct((3, 1, hb, wb), f32),
            jax.ShapeDtypeStruct((3, 1, hb, wb), f32),
        ),
        in_specs=[vm] * 5,
        out_specs=(vm, vm, vm),
        compiler_params=pltpu.CompilerParams(vmem_limit_bytes=60 * 1024 * 1024),
    )(*near, dual)


def solution(mesh):
    placed = (
        P("depth", "row", "col"),
        P(None, "depth", "row", "col"),
        P("row", "col"),
        P(None, "depth", "row", "col"),
    )
    return jax.shard_map(
        functools.partial(shards, mesh.shape["depth"], mesh.shape["row"], mesh.shape["col"]),
        mesh=mesh,
        in_specs=placed,
        out_specs=(
            P("depth", "row", "col"),
            P(None, "depth", "row", "col"),
            P(None, "depth", "row", "col"),
        ),
        check_vma=False,
    )
```

```python
import functools

import jax
import jax.numpy as jnp
import numpy as np
from jax import lax
from jax.experimental import pallas as pl
from jax.experimental.pallas import tpu as pltpu
from jax.sharding import PartitionSpec as P

step_size = 1.0
shrink_level = 0.5
MESH = pl.DeviceIdType.MESH


def dot_of(a, b, side):
    return lax.dot_general(a, b, (((1,), (side,)), ((), ())), preferred_element_type=jnp.float32)


def halves(a):
    high = a.astype(jnp.bfloat16)
    return high, (a - high.astype(jnp.float32)).astype(jnp.bfloat16)


def dot_right(a, table, side):
    high, low = halves(a)
    return dot_of(high, table[0], side) + (dot_of(high, table[1], side) + dot_of(low, table[0], side))


def dot_left(table, b):
    high, low = b
    return dot_of(table[0], high, 0) + (dot_of(table[0], low, 0) + dot_of(table[1], high, 0))


def root(count, n):
    value = np.exp(-2j * np.pi * (n % count) / count)
    real, imag = float(value.real), float(value.imag)
    real = round(real) if abs(real - round(real)) < 1e-12 else real
    imag = round(imag) if abs(imag - round(imag)) < 1e-12 else imag
    return float(real), float(imag)


def add_scaled(total, scale, value):
    if scale == 0.0:
        return total
    if total is None:
        return value if scale == 1.0 else (-value if scale == -1.0 else scale * value)
    if scale == 1.0:
        return total + value
    if scale == -1.0:
        return total - value
    return total + scale * value


def spin(u):
    half = u.shape[-1] // 2
    lane = lax.broadcasted_iota(jnp.int32, u.shape, u.ndim - 1)
    rolled = pltpu.roll(u, half, u.ndim - 1)
    return jnp.where(lane < half, -rolled, rolled)


def body(D, R, C, hb, wb,
         vol, psf, meas, mat_w, mat_h, tw_w, tw_h,
         out_u, out_dep, out_row, out_col,
         r_vol, k_send, k_recv, r_meas, s1, r1, s2, r2, s3, r3, s4, r4, s5, r5, ups, h_dep, h_row, h_col, edge,
         sm_vol, sm_k, sm_meas, sm1, sm2s, sm2r, sm3s, sm3r, sm4, sm5, sm_h, sm_dep):
    H, W = R * hb, C * wb
    rows, q = hb // C, wb // R
    rs = rows // D
    lo, hi, lo_c, hi_c = R // 4, 3 * R // 4, C // 4, 3 * C // 4
    NR = hi - lo
    N, n16, NO = D * R * C, R * C, D * NR * C
    d, r, c = lax.axis_index("depth"), lax.axis_index("row"), lax.axis_index("col")
    me16 = r * C + c
    me = d * n16 + me16

    def ids(t):
        return {"depth": t // n16, "row": (t // C) % R, "col": t % C}

    barrier = pltpu.get_barrier_semaphore()

    def greet(o, _):
        pl.semaphore_signal(barrier, inc=1, device_id=ids(lax.rem(me + o, N)), device_id_type=MESH)
        return 0

    lax.fori_loop(1, N, greet, 0)

    def rc(src, dst, ss, rsm, dev):
        return pltpu.make_async_remote_copy(src_ref=src, dst_ref=dst, send_sem=ss, recv_sem=rsm, device_id=dev, device_id_type=MESH)

    def loop(lower, upper, f):
        def g(i, x):
            f(i)
            return x
        lax.fori_loop(lower, upper, g, 0)

    far_cols = sorted(range(C), key=lambda k: (k == 0, abs(k - C // 2)))
    far_first = [(co, ro) for co in far_cols for ro in range(R)]

    class A2A:
        def __init__(self, n, pos, dev, src, recv, sems):
            self.n, self.pos, self.dev, self.src, self.recv, self.sems = n, pos, dev, src, recv, sems

        def start(self):
            def go(o):
                t = lax.rem(self.pos + o, self.n)
                rc(self.src(t), self.recv(self.pos), self.sems.at[0, t], self.sems.at[1, self.pos], self.dev(t)).start()
            if self.n == R:
                loop(1, self.n, go)
                return
            for co, ro in far_first:
                t = lax.rem(r + ro, R) * C + lax.rem(c + co, C)
                if (co, ro) != (0, 0):
                    rc(self.src(t), self.recv(self.pos), self.sems.at[0, t], self.sems.at[1, self.pos], self.dev(t)).start()

        def wait(self):
            def go(o):
                t = lax.rem(self.pos + o, self.n)
                rc(self.src(t), self.recv(t), self.sems.at[0, t], self.sems.at[1, t], self.dev(t)).wait()
            loop(1, self.n, go)

    col_dev = lambda t: {"col": t}
    row_dev = lambda t: {"row": t}
    all_dev = lambda t: {"row": t // C, "col": lax.rem(t, C)}

    half = rows // 2

    def in_halves(n, pos, dev, send, recv, sems):
        def one(h):
            part = slice(h * half, (h + 1) * half)
            return A2A(n, pos, dev, lambda t: send.at[t, part], lambda t: recv.at[t, part], sems.at[h])
        return [one(0), one(1)]

    x_vol = in_halves(C, c, col_dev, vol, r_vol, sm_vol)
    x_k = A2A(R, r, row_dev, lambda t: k_send.at[t], lambda t: k_recv.at[t], sm_k)
    x_meas = A2A(C, c, col_dev, lambda t: meas.at[t, d], lambda t: r_meas.at[t], sm_meas)
    x1 = in_halves(n16, me16, all_dev, s1, r1, sm1)
    x4 = in_halves(n16, me16, all_dev, s4, r4, sm4)
    x5 = in_halves(C, c, col_dev, s5, r5, sm5)

    pl.semaphore_wait(barrier, N - 1)
    x_vol[0].start()
    x_vol[1].start()
    r_vol[c] = vol[c]

    kin = jnp.concatenate([psf[0], psf[1]], axis=1)
    i0 = lax.broadcasted_iota(jnp.int32, (2 * wb, 2 * wb), 0)
    i1 = lax.broadcasted_iota(jnp.int32, (2 * wb, 2 * wb), 1)
    target = (lax.rem(i1, 2 * q) // q) * wb + R * lax.rem(i1, q) + i1 // (2 * q)
    perm_c = jnp.where(i0 == target, 1.0, 0.0).astype(jnp.float32)
    j0 = lax.broadcasted_iota(jnp.int32, (hb, hb), 0)
    j1 = lax.broadcasted_iota(jnp.int32, (hb, hb), 1)
    t_rows = hb // R
    perm_r = jnp.where(j1 == R * lax.rem(j0, t_rows) + j0 // t_rows, 1.0, 0.0).astype(jnp.float32)
    perm_c, perm_r = perm_c.astype(jnp.bfloat16), perm_r.astype(jnp.bfloat16)
    kin_high, kin_low = halves(kin)
    kk = (dot_of(perm_r, dot_of(kin_high, perm_c, 0).astype(jnp.bfloat16), 0)
          + dot_of(perm_r, dot_of(kin_low, perm_c, 0).astype(jnp.bfloat16), 0))
    for j in range(R):
        k_send[j] = kk[:, 2 * q * j:2 * q * (j + 1)]
    x_k.start()
    k_recv[r] = k_send[r]
    x_meas.start()
    r_meas[c] = meas[c, d]

    def fwd_w(blocks, first):
        tre, tim = [], []
        for k1 in range(C):
            yr = yi = None
            for i, blk in enumerate(blocks):
                a, b = root(C, (first + i) * k1)
                yr, yi = add_scaled(yr, a, blk), add_scaled(yi, b, blk)
            ct, st = tw_w[0, k1:k1 + 1, :], tw_w[1, k1:k1 + 1, :]
            if yi is None:
                tre.append(yr * ct)
                tim.append(yr * st)
            else:
                tre.append(yr * ct - yi * st)
                tim.append(yr * st + yi * ct)
        both = jnp.concatenate([jnp.concatenate(tre, 0), jnp.concatenate(tim, 0)], 1)
        return dot_right(both, (mat_w[0], mat_w[1]), 0)

    def inv_w(z, count, first, last):
        g = dot_right(z, (mat_w[0], mat_w[1]), 1) * (1.0 / W)
        gr, gi = [], []
        for k1 in range(C):
            a = g[k1 * count:(k1 + 1) * count, :wb]
            b = g[k1 * count:(k1 + 1) * count, wb:]
            ct, st = tw_w[0, k1:k1 + 1, :], tw_w[1, k1:k1 + 1, :]
            gr.append(a * ct + b * st)
            gi.append(b * ct - a * st)
        out = []
        for n1 in range(first, last):
            total = None
            for k1 in range(C):
                a, b = root(C, n1 * k1)
                total = add_scaled(total, a, gr[k1])
                total = add_scaled(total, b, gi[k1])
            out.append(total)
        return out

    def fwd_h(us, first):
        vs = [spin(u) for u in us]
        tu, tv = [], []
        for k1 in range(R):
            yu = yv = None
            for i in range(len(us)):
                a, b = root(R, (first + i) * k1)
                yu = add_scaled(add_scaled(yu, a, us[i]), b, vs[i])
                yv = add_scaled(add_scaled(yv, a, vs[i]), -b, us[i])
            ct, st = tw_h[:, k1:k1 + 1], tw_h[:, R + k1:R + k1 + 1]
            tu.append(yu * ct + yv * st)
            tv.append(yv * ct - yu * st)
        return (dot_left((mat_h[0, 0], mat_h[1, 0]), halves(jnp.concatenate(tu, 1)))
                + dot_left((mat_h[0, 1], mat_h[1, 1]), halves(jnp.concatenate(tv, 1))))

    def inv_h(ps, first, last):
        vs = [spin(p) for p in ps]
        g = (dot_left((mat_h[0, 0], mat_h[1, 0]), halves(jnp.concatenate(ps, 1)))
             - dot_left((mat_h[0, 1], mat_h[1, 1]), halves(jnp.concatenate(vs, 1)))) * (1.0 / H)
        gu, gv = [], []
        for k1 in range(R):
            u = g[:, 2 * q * k1:2 * q * (k1 + 1)]
            v = spin(u)
            ct, st = tw_h[:, k1:k1 + 1], tw_h[:, R + k1:R + k1 + 1]
            gu.append(u * ct - v * st)
            gv.append(v * ct + u * st)
        out = []
        for n1 in range(first, last):
            total = None
            for k1 in range(R):
                a, b = root(R, n1 * k1)
                total = add_scaled(add_scaled(total, a, gu[k1]), -b, gv[k1])
            out.append(total)
        return out

    def kernel_parts(k1):
        k = jnp.concatenate([k_recv[j, k1 * t_rows:(k1 + 1) * t_rows, :] for j in range(R)], 0)
        rolled = pltpu.roll(k, q, 1)
        lane = lax.broadcasted_iota(jnp.int32, k.shape, 1)
        return jnp.where(lane < q, k, rolled), jnp.where(lane < q, rolled, k)

    for h in range(2):
        part = slice(h * half, (h + 1) * half)
        x_vol[h].wait()
        z = fwd_w([r_vol[j, part] for j in range(C)], 0)
        for k1 in range(R):
            for j in range(C):
                s1[k1 * C + j, part] = z[k1 * half:(k1 + 1) * half, 2 * q * j:2 * q * (j + 1)]
        x1[h].start()
    r1[me16] = s1[me16]
    x1[0].wait()
    x1[1].wait()
    x_k.wait()

    def joined(ref, first, count):
        return jnp.concatenate([ref[first + j] for j in range(count)], 0)

    s = fwd_h([joined(r1, j * C, C) for j in range(R)], 0)
    ps = []
    for k1 in range(R):
        kr, ki = kernel_parts(k1)
        u = s[:, 2 * q * k1:2 * q * (k1 + 1)]
        ps.append(kr * u + ki * spin(u))
    xs = inv_h(ps, lo, hi)

    for i in range(NR):
        for j in range(C):
            for e in range(D):
                s2[(e * NR + i) * C + j] = xs[i][j * rows + e * rs:j * rows + (e + 1) * rs, :]

    def owner_id(t):
        return (t // (NR * C)) * n16 + (lo + (t // C) % NR) * C + t % C

    def send2(o, co):
        t = lax.rem(d * NR + r + o, D * NR) * C + lax.rem(c + co, C)
        w = owner_id(t)

        @pl.when(w != me)
        def _():
            rc(s2.at[t], r2.at[me], sm2s.at[t], sm2r.at[me], ids(w)).start()

        @pl.when(w == me)
        def _():
            r2[me] = s2[t]

    for co in far_cols:
        loop(0, D * NR, functools.partial(send2, co=co))
    x_meas.wait()
    is_owner = (r >= lo) & (r < hi)
    my_owner = ((r - lo) * C + c) * D + d

    @pl.when(is_owner)
    def _():
        def wait2(o):
            t = lax.rem(me + o, N)
            rc(r2.at[t], r2.at[t], sm2s.at[0], sm2r.at[t], ids(t)).wait_recv()

        loop(1, N, wait2)
        zs = []
        for k1 in range(R):
            pieces = []
            for j in range(C):
                total = r2[k1 * C + j]
                for e in range(1, D):
                    total = total + r2[e * n16 + k1 * C + j]
                pieces.append(total)
            zs.append(jnp.concatenate(pieces, 1))
        sensor = inv_w(jnp.concatenate(zs, 0), rs, lo_c, hi_c)
        res = [sensor[i] - r_meas[lo_c + i] for i in range(hi_c - lo_c)]
        zz = fwd_w(res, lo_c)
        for k1 in range(R):
            for j in range(C):
                s3[k1 * C + j] = zz[k1 * rs:(k1 + 1) * rs, 2 * q * j:2 * q * (j + 1)]

        def send3(o, co, ro):
            t = lax.rem(d + o, D) * n16 + lax.rem(r + ro, R) * C + lax.rem(c + co, C)
            rc(s3.at[lax.rem(t, n16)], r3.at[my_owner], sm3s.at[t], sm3r.at[my_owner], ids(t)).start()

        for co, ro in far_first:
            loop(1 if (co, ro) == (0, 0) else 0, D, functools.partial(send3, co=co, ro=ro))
        r3[my_owner] = s3[me16]

        def drain3(o):
            t = lax.rem(me + o, N)
            rc(s3.at[lax.rem(t, n16)], r3.at[my_owner], sm3s.at[t], sm3r.at[my_owner], ids(t)).wait_send()

        loop(1, N, drain3)

    def drain2(o):
        t = lax.rem(me + o, NO)
        w = owner_id(t)

        @pl.when(w != me)
        def _():
            rc(s2.at[t], r2.at[me], sm2s.at[t], sm2r.at[me], ids(w)).wait_send()

    loop(0, NO, drain2)

    def wait3(t):
        w = (t % D) * n16 + (lo + t // (C * D)) * C + (t // D) % C

        @pl.when(w != me)
        def _():
            rc(r3.at[t], r3.at[t], sm3s.at[0], sm3r.at[t], ids(w)).wait_recv()

    loop(0, NO, wait3)
    s = fwd_h([joined(r3, i * C * D, C * D) for i in range(NR)], lo)
    ps = []
    for k1 in range(R):
        kr, ki = kernel_parts(k1)
        u = s[:, 2 * q * k1:2 * q * (k1 + 1)]
        ps.append(kr * u - ki * spin(u))
    xs = inv_h(ps, 0, R)
    for i in range(R):
        for j in range(C):
            s4[i * C + j] = xs[i][j * rows:(j + 1) * rows, :]
    x4[0].start()
    x4[1].start()
    r4[me16] = s4[me16]
    for h in range(2):
        part = slice(h * half, (h + 1) * half)
        x4[h].wait()
        zs = [jnp.concatenate([r4[k1 * C + j, part] for j in range(C)], 1) for k1 in range(R)]
        adj = inv_w(jnp.concatenate(zs, 0), half, 0, C)
        for j in range(C):
            s5[j, part] = adj[j]
        x5[h].start()
    down_d, down_r, down_c = lax.rem(d + D - 1, D), lax.rem(r + R - 1, R), lax.rem(c + C - 1, C)
    far = d > 0

    def plane_copy(t, h, to):
        part = slice(h * half, (h + 1) * half)
        return rc(ups.at[t, part], h_dep.at[t, part], sm_dep.at[h, 0, t], sm_dep.at[h, 1, t], {"depth": to})

    for h in range(2):
        part = slice(h * half, (h + 1) * half)

        def take(t, value):
            ups[t, part] = vol[t, part] - step_size * value

            @pl.when(far)
            def _():
                plane_copy(t, h, d - 1).start()

        take(c, s5[c, part])

        def arrive(o):
            t = lax.rem(c + o, C)
            rc(s5.at[t, part], r5.at[t, part], sm5.at[h, 0, t], sm5.at[h, 1, t], col_dev(t)).wait()
            take(t, r5[t, part])

        loop(1, C, arrive)
    for j in range(C):
        edge[j * rows:(j + 1) * rows, :] = ups[j, :, 0:128]
    copies = [
        rc(ups.at[0, 0:8, :], h_row, sm_h.at[0, 0], sm_h.at[1, 0], {"row": down_r}),
        rc(edge, h_col, sm_h.at[0, 1], sm_h.at[1, 1], {"col": down_c}),
    ]
    for cp in copies:
        cp.start()
    for j in range(C):
        out_u[j * rows:(j + 1) * rows, :] = ups[j]
    copies[0].wait()
    out_row[...] = h_row[...]
    copies[1].wait()
    out_col[...] = h_col[...]

    @pl.when(far)
    def _():
        def sent(t):
            plane_copy(t, 0, d - 1).wait_send()
            plane_copy(t, 1, d - 1).wait_send()

        loop(0, C, sent)

    @pl.when(d < D - 1)
    def _():
        def landed(t):
            plane_copy(t, 0, d + 1).wait_recv()
            plane_copy(t, 1, d + 1).wait_recv()

        loop(0, C, landed)
        for j in range(C):
            out_dep[j * rows:(j + 1) * rows, :] = h_dep[j]

    @pl.when(d == D - 1)
    def _():
        for j in range(C):
            out_dep[j * rows:(j + 1) * rows, :] = ups[j]


def tail(D, R, C, ups, dep, row, col, dual, upd, shr, dnx):
    hb, wb = ups.shape
    r, c = lax.axis_index("row"), lax.axis_index("col")
    u = ups[...]
    upd[0] = u

    def finish(i, diff):
        combined = diff + dual[i, 0]
        clipped = jnp.clip(combined, -shrink_level, shrink_level)
        shr[i, 0] = combined - clipped
        dnx[i, 0] = clipped

    finish(0, dep[...] - u)
    rid = lax.broadcasted_iota(jnp.int32, (hb, wb), 0)
    nxt = jnp.where(rid == hb - 1, jnp.broadcast_to(row[0:1, :], (hb, wb)), pltpu.roll(u, hb - 1, 0))
    finish(1, jnp.where(r * hb + rid < hb * R - 1, nxt - u, 0.0))
    cid = lax.broadcasted_iota(jnp.int32, (hb, wb), 1)
    nxt = jnp.where(cid == wb - 1, jnp.broadcast_to(col[:, 0:1], (hb, wb)), pltpu.roll(u, wb - 1, 1))
    finish(2, jnp.where(c * wb + cid < wb * C - 1, nxt - u, 0.0))


def two_halves(table):
    high = table.astype(jnp.bfloat16)
    return np.stack([high, (table - high.astype(np.float64)).astype(jnp.bfloat16)])


def shards(D, R, C, volume, psf_spec, measured, dual):
    planes, hb, wb = volume.shape
    assert planes == 1 and R == C
    H, W = hb * R, wb * C
    rows, q = hb // C, wb // R
    rs = rows // D
    NO, N, n16 = D * (3 * R // 4 - R // 4) * C, D * R * C, R * C
    n2, k2 = np.arange(wb), np.arange(wb)
    f = np.exp(-2j * np.pi * ((n2[:, None] * k2[None]) % wb) / wb).reshape(wb, C, 1, wb // C)
    top = np.concatenate([f.real, f.imag], 2).reshape(wb, 2 * wb)
    bot = np.concatenate([-f.imag, f.real], 2).reshape(wb, 2 * wb)
    mat_w = two_halves(np.concatenate([top, bot], 0))
    m = np.arange(hb)
    g = np.exp(-2j * np.pi * ((m[:, None] * m[None]) % hb) / hb)
    mat_h = two_halves(np.stack([g.real, g.imag]))
    t = np.exp(-2j * np.pi * (np.arange(C)[:, None] * n2[None]) / W)
    tw_w = np.stack([t.real, t.imag]).astype(np.float32)
    t = np.exp(-2j * np.pi * (m[:, None] * np.arange(R)[None]) / H)
    tw_h = np.concatenate([t.real, t.imag], 1).astype(np.float32)
    f32 = jnp.float32
    V = pltpu.VMEM
    dma = pltpu.SemaphoreType.DMA
    vm = pl.BlockSpec(memory_space=pltpu.VMEM)
    near = pl.pallas_call(
        functools.partial(body, D, R, C, hb, wb),
        name="admm",
        out_shape=(
            jax.ShapeDtypeStruct((hb, wb), f32),
            jax.ShapeDtypeStruct((hb, wb), f32),
            jax.ShapeDtypeStruct((8, wb), f32),
            jax.ShapeDtypeStruct((hb, 128), f32),
        ),
        in_specs=[vm] * 7,
        out_specs=(vm, vm, vm, vm),
        scratch_shapes=[
            V((C, rows, wb), f32),
            V((R, hb, 2 * q), f32), V((R, hb, 2 * q), f32),
            V((C, rs, wb), f32),
            V((n16, rows, 2 * q), f32), V((n16, rows, 2 * q), f32),
            V((NO, rs, 2 * q), f32), V((N, rs, 2 * q), f32),
            V((n16, rs, 2 * q), f32), V((NO, rs, 2 * q), f32),
            V((n16, rows, 2 * q), f32), V((n16, rows, 2 * q), f32),
            V((C, rows, wb), f32), V((C, rows, wb), f32),
            V((C, rows, wb), f32), V((C, rows, wb), f32), V((8, wb), f32), V((hb, 128), f32), V((hb, 128), f32),
            dma((2, 2, C)), dma((2, R)), dma((2, C)), dma((2, 2, n16)), dma((NO,)), dma((N,)),
            dma((N,)), dma((NO,)), dma((2, 2, n16)), dma((2, 2, C)), dma((2, 2)), dma((2, 2, C)),
        ],
        compiler_params=pltpu.CompilerParams(
            collective_id=0, has_side_effects=True, vmem_limit_bytes=60 * 1024 * 1024
        ),
    )(
        volume.reshape(C, rows, wb), psf_spec.reshape(2, hb, wb), measured.reshape(C, D, rs, wb),
        jnp.asarray(mat_w), jnp.asarray(mat_h), jnp.asarray(tw_w), jnp.asarray(tw_h),
    )
    return pl.pallas_call(
        functools.partial(tail, D, R, C),
        name="tail",
        out_shape=(
            jax.ShapeDtypeStruct((1, hb, wb), f32),
            jax.ShapeDtypeStruct((3, 1, hb, wb), f32),
            jax.ShapeDtypeStruct((3, 1, hb, wb), f32),
        ),
        in_specs=[vm] * 5,
        out_specs=(vm, vm, vm),
        compiler_params=pltpu.CompilerParams(vmem_limit_bytes=60 * 1024 * 1024),
    )(*near, dual)


def solution(mesh):
    placed = (
        P("depth", "row", "col"),
        P(None, "depth", "row", "col"),
        P("row", "col"),
        P(None, "depth", "row", "col"),
    )
    return jax.shard_map(
        functools.partial(shards, mesh.shape["depth"], mesh.shape["row"], mesh.shape["col"]),
        mesh=mesh,
        in_specs=placed,
        out_specs=(
            P("depth", "row", "col"),
            P(None, "depth", "row", "col"),
            P(None, "depth", "row", "col"),
        ),
        check_vma=False,
    )
```
